128 devices in a mesh: seq: 32 (over z, x_lo, y), chan: 4 (over x_hi, core).
Axes of the slice: x: 4 (x_hi: 2, x_lo: 2; x = x_hi * 2 + x_lo), y: 4, z: 4, core: 2. Of those that a mesh axis runs over, the one named last changes fastest.
Arguments:
- tokens: bfloat16 [32768, 512], P('seq', 'chan'), may hold values from -6 to 6
- w_in: bfloat16 [512, 3, 512], P(None, None, 'chan'), may hold values from -0.25 to 0.25
- short_filter: float32 [3, 3, 512], P(None, None, 'chan'), may hold values from -3 to 3
- long_filter: float32 [32768, 512], P('seq', 'chan'), may hold values from -0.03125 to 0.03125
- skip_gain: float32 [512], P('chan'), may hold values from 0.5 to 1.5
- w_out: bfloat16 [512, 512], P('chan'), may hold values from -0.25 to 0.25
Outputs:
- mixed: bfloat16 [32768, 512], P('seq', 'chan')
The draws below stay inside these ranges and needn't reach their ends.
All inputs are finite; a program needn't handle non-finite values.
Results may differ from the reference program's by a relative error of at most 0.007.
Values may be sent and summed in bfloat16 or wider, within the bound.
No kernel may reach another device: no remote copies, remote signals or barrier semaphores. Data moves between devices by JAX's collectives and lax.ppermute only.
A program may use at most 64 MiB of HBM per device.

```python
import jax
import jax.numpy as jnp

C = 512
L = 32768


def block_scale(rng, dims, shards, low, high):
    def one(dim, shards_of):
        steps = jax.random.uniform(jax.random.fold_in(jax.random.fold_in(rng, 6), dim), (shards_of,), jnp.float32, low / len(shards), high / len(shards))
        return jnp.repeat(jnp.exp(steps), dims[dim] // shards_of).reshape((-1,) + (1,) * (len(dims) - dim - 1))

    factor_of = one(*shards[0])
    for cut in shards[1:]:
        factor_of = factor_of * one(*cut)
    return factor_of


def scatter_about(own_key, dims, scale, limit, shards=(), kind=jnp.bfloat16):
    loudness = block_scale(own_key, dims, shards, -0.22, 0.18) if shards else 1.0
    drawn = jax.random.normal(own_key, dims, jnp.float32) * scale * loudness
    return jnp.minimum(jnp.maximum(drawn, -limit), limit).astype(kind)


def setup_inputs(seed: int = 0) -> dict:
    splits = jax.random.split(jax.random.key(seed), 7)
    tokens = scatter_about(splits[0], (L, C), 1.0, 6.0, ((0, 32), (1, 4)))
    w_in = scatter_about(splits[1], (C, 3, C), C ** -0.5, 0.25, ((2, 4),))
    short_filter = scatter_about(splits[2], (3, 3, C), 0.6, 3.0, ((2, 4),), jnp.float32)
    long_filter = scatter_about(splits[3], (L, C), L ** -0.5, 0.03125, ((0, 32), (1, 4)), jnp.float32)
    skip_gain = jnp.clip(0.5 + 1.0 * jax.random.uniform(splits[4], (C,), jnp.float32) ** block_scale(splits[4], (C,), ((0, 4),), -0.2, 0.2), 0.5, 1.5)
    w_out = scatter_about(splits[5], (C, C), C ** -0.5, 0.25, ((0, 4),))
    return {"tokens": tokens, "w_in": w_in, "short_filter": short_filter, "long_filter": long_filter, "skip_gain": skip_gain, "w_out": w_out}


def reference(tokens, w_in, short_filter, long_filter, skip_gain, w_out):
    width = tokens.shape[1]
    length = tokens.shape[0]
    projected = jnp.dot(tokens, w_in.reshape(width, 3 * width), preferred_element_type=jnp.float32)
    projected = projected.astype(jnp.bfloat16).reshape(length, 3, width)
    padded = jnp.concatenate([jnp.zeros((2, 3, width), jnp.float32), projected.astype(jnp.float32)], axis=0)
    short = short_filter[0] * padded[2:] + short_filter[1] * padded[1:-1] + short_filter[2] * padded[:-2]
    inner = short[:, 0, :] * short[:, 1, :]
    spectrum = jnp.fft.rfft(inner, n=2 * length, axis=0) * jnp.fft.rfft(long_filter, n=2 * length, axis=0)
    conv = jnp.fft.irfft(spectrum, n=2 * length, axis=0)[:length]
    gated = (short[:, 2, :] * (conv + skip_gain * inner)).astype(jnp.bfloat16)
    return jnp.dot(gated, w_out, preferred_element_type=jnp.float32).astype(jnp.bfloat16)
```

```python
import functools
import math

import jax
import jax.numpy as jnp
import ml_dtypes
import numpy as np
from jax import lax
from jax.experimental import pallas as pl
from jax.experimental.pallas import tpu as pltpu
from jax.sharding import PartitionSpec as P


F32 = jnp.float32
BF16 = jnp.bfloat16
VMEM = pltpu.VMEM

SHARDS = 32
CHANS = 4
ROWS = 1024
WIDTH = 128
GROUP = 4
OUTER = 256
INNER = 128
LENGTH = OUTER * INNER


def halves(table):
    high = table.astype(ml_dtypes.bfloat16)
    low = (table - high.astype(np.float64)).astype(ml_dtypes.bfloat16)
    return high, low


@functools.lru_cache(None)
def tables():
    k1 = np.arange(OUTER)[:, None]
    a = np.arange(OUTER)[None, :]
    angle = 2 * math.pi / (4 * OUTER) * (a * (4 * k1 + 1) % (4 * OUTER))
    first = np.concatenate([np.cos(angle), -np.sin(angle)], 0)
    last = np.concatenate([np.cos(angle), -np.sin(angle)], 0).T / LENGTH
    p = np.arange(INNER)
    turn = 2 * math.pi / (4 * LENGTH) * (p[None, :] * (4 * k1 + 1) % (4 * LENGTH))
    twiddle = np.concatenate([np.cos(turn), np.sin(turn)], 1).astype(np.float32)
    phase = 2 * math.pi / INNER * (p[:, None] * p[None, :] % INNER)
    c, s = np.cos(phase), np.sin(phase)
    second = np.block([[c, -s], [s, c]])
    third = np.block([[c, s], [-s, c]])
    return twiddle, halves(first), halves(second), halves(third), halves(last)


def split(value):
    high = value.astype(BF16)
    return high, (value - high.astype(F32)).astype(BF16)


def dot(left, right):
    return jnp.dot(left, right, preferred_element_type=F32)


def dot3(left, right):
    (lh, ll), (rh, rl) = left, right
    return dot(lh, rh) + (dot(lh, rl) + dot(ll, rh))


def load_signal(ref):
    wide = ref[...].astype(F32).reshape(SHARDS, GROUP, 8, INNER)
    return jnp.concatenate(
        [wide[:, c].reshape(OUTER, INNER).astype(BF16) for c in range(GROUP)], axis=1
    )


def forward(signal, tw, f_hi, f_lo, s_hi, s_lo):
    first = dot(f_hi[...], signal) + dot(f_lo[...], signal)
    cos, sin = tw[:, :INNER], tw[:, INNER:]
    rows = []
    for c in range(GROUP):
        re = first[:OUTER, c * INNER : (c + 1) * INNER]
        im = first[OUTER:, c * INNER : (c + 1) * INNER]
        rows.append(jnp.concatenate([re * cos + im * sin, im * cos - re * sin], axis=1))
    turned = jnp.concatenate(rows, axis=0)
    return dot3(split(turned), (s_hi[...], s_lo[...]))


def filter_kernel(sig, tw, f_hi, f_lo, s_hi, s_lo, out):
    out[...] = forward(load_signal(sig), tw, f_hi, f_lo, s_hi, s_lo)


def conv_kernel(sig, spec, tw, f_hi, f_lo, s_hi, s_lo, t_hi, t_lo, l_hi, l_lo, out):
    mine = forward(load_signal(sig), tw, f_hi, f_lo, s_hi, s_lo)
    mr, mi = mine[:, :INNER], mine[:, INNER:]
    hr, hi = spec[:, :INNER], spec[:, INNER:]
    product = jnp.concatenate([mr * hr - mi * hi, mr * hi + mi * hr], axis=1)
    back = dot3(split(product), (t_hi[...], t_lo[...]))
    cos, sin = tw[:, :INNER], tw[:, INNER:]
    res, ims = [], []
    for c in range(GROUP):
        re = back[c * OUTER : (c + 1) * OUTER, :INNER]
        im = back[c * OUTER : (c + 1) * OUTER, INNER:]
        res.append(re * cos - im * sin)
        ims.append(im * cos + re * sin)
    turned = jnp.concatenate(
        [jnp.concatenate(res, axis=1), jnp.concatenate(ims, axis=1)], axis=0
    )
    y = dot3((l_hi[...], l_lo[...]), split(turned))
    parts = [
        y[:, c * INNER : (c + 1) * INNER].reshape(SHARDS, 1, 8, INNER) for c in range(GROUP)
    ]
    wide = jnp.concatenate(parts, axis=1).reshape(SHARDS, GROUP * 8, INNER)
    out[...] = wide.astype(BF16)


def to_channels(value, scratch, out):
    for q in range(8):
        scratch[pl.ds(q, WIDTH, stride=8), :] = value[q * INNER : (q + 1) * INNER].T
    out[...] = scratch[...].reshape(SHARDS, GROUP * 8, INNER).astype(BF16)


def turn_kernel(value, out, scratch):
    to_channels(value[...], scratch, out)


def project_kernel(me, t0, t1, t2, t3, r0, r1, r2, r3, w, short_filter, skip, out, gate, direct, ext, scratch):
    chan = me[0]
    first = me[1] == 0
    weights = jnp.concatenate(
        [w[pl.ds(pl.multiple_of((chan ^ r) * WIDTH, WIDTH), WIDTH), :] for r in range(CHANS)], axis=0
    )
    rim = jnp.concatenate([r0[...], r1[...], r2[...], r3[...]], axis=1)
    rim = dot(rim, weights).astype(BF16).astype(F32)
    ext[:8, :] = jnp.where(first, 0.0, rim[:8])
    tokens = jnp.concatenate([t0[...], t1[...], t2[...], t3[...]], axis=1)
    ext[8:, :] = dot(tokens, weights).astype(BF16).astype(F32)
    short = []
    for g in range(3):
        lanes = slice(g * WIDTH, (g + 1) * WIDTH)
        taps = [short_filter[j, g, :].reshape(1, WIDTH) for j in range(3)]
        short.append(
            taps[0] * ext[8:, lanes]
            + taps[1] * ext[7 : ROWS + 7, lanes]
            + taps[2] * ext[6 : ROWS + 6, lanes]
        )
    inner = short[0] * short[1]
    gate[...] = short[2]
    direct[...] = skip[...] * inner
    to_channels(inner, scratch, out)


def gate_kernel(conv, gate, direct, out, scratch):
    scratch[...] = conv[...].astype(F32).reshape(ROWS, WIDTH)
    for q in range(8):
        rows = slice(q * INNER, (q + 1) * INNER)
        back = scratch[pl.ds(q, WIDTH, stride=8), :].T
        out[rows, :] = (gate[rows, :] * (back + direct[rows, :])).astype(BF16)


def output_kernel(g0, g1, g2, g3, w0, w1, w2, w3, out):
    gated = jnp.concatenate([g0[...], g1[...], g2[...], g3[...]], axis=1)
    weights = jnp.concatenate([w0[...], w1[...], w2[...], w3[...]], axis=0)
    out[...] = dot(gated, weights).astype(BF16)


def call(kernel, out_shape, args, scratch=(), smem=0, flops=0, name=None):
    many = isinstance(out_shape, (list, tuple))
    specs = [pl.BlockSpec(memory_space=pltpu.SMEM)] * smem
    specs += [pl.BlockSpec(memory_space=VMEM)] * (len(args) - smem)
    outs = [pl.BlockSpec(memory_space=VMEM) for _ in out_shape] if many else pl.BlockSpec(memory_space=VMEM)
    moved = sum(x.size * x.dtype.itemsize for x in args)
    return pl.pallas_call(
        kernel,
        out_shape=out_shape,
        in_specs=specs,
        out_specs=outs,
        scratch_shapes=list(scratch),
        name=name,
        cost_estimate=pl.CostEstimate(flops=flops, bytes_accessed=moved, transcendentals=0),
        compiler_params=pltpu.CompilerParams(vmem_limit_bytes=48 << 20),
    )(*args)


def swap(value, distance):
    return lax.ppermute(value, "chan", [(i, i ^ distance) for i in range(CHANS)])


def gather(value):
    near = swap(value, 1)
    far = swap(value, 2)
    return [value, near, far, swap(far, 1)]


def on_device(tokens, w_in, short_filter, long_filter, skip_gain, w_out):
    chan = lax.axis_index("chan")
    shard = lax.axis_index("seq")
    me = jnp.stack([chan, shard]).astype(jnp.int32)
    packed = jax.ShapeDtypeStruct((SHARDS, GROUP * 8, INNER), BF16)
    turned = VMEM((ROWS, WIDTH), F32)
    block = jax.ShapeDtypeStruct((ROWS, WIDTH), F32)

    tw, first, second, third, last = tables()
    tw = jnp.asarray(tw)
    first, second, third, last = [tuple(jnp.asarray(x) for x in t) for t in (first, second, third, last)]

    blocks = gather(tokens)
    rims = []
    for r in range(CHANS):
        route = [
            (s * CHANS + c, (s + 1) * CHANS + (c ^ r)) for s in range(SHARDS - 1) for c in range(CHANS)
        ]
        rims.append(lax.ppermute(tokens[-8:], ("seq", "chan"), route))
    columns = []
    for r in range(CHANS):
        piece = lax.dynamic_slice_in_dim(w_out, (chan ^ r) * WIDTH, WIDTH, axis=1)
        columns.append(piece if r == 0 else swap(piece, r))

    taps = call(turn_kernel, packed, [long_filter], [turned], name="turn")
    taps = lax.all_to_all(taps, "seq", 0, 0)
    spec = call(
        filter_kernel,
        jax.ShapeDtypeStruct((GROUP * OUTER, 2 * INNER), F32),
        [taps, tw, *first, *second],
        flops=2 * 332 << 20,
        name="filter",
    )

    inner, gate, direct = call(
        project_kernel,
        [packed, block, block],
        [me, *blocks, *rims, w_in.reshape(CHANS * WIDTH, 3 * WIDTH), short_filter, skip_gain.reshape(1, WIDTH)],
        [VMEM((ROWS + 8, 3 * WIDTH), F32), turned],
        smem=1,
        flops=2 * 200 << 20,
        name="project",
    )
    inner = lax.all_to_all(inner, "seq", 0, 0)
    conv = call(
        conv_kernel, packed, [inner, spec, tw, *first, *second, *third, *last], flops=2 * 728 << 20, name="conv"
    )
    conv = lax.all_to_all(conv, "seq", 0, 0)
    gated = call(
        gate_kernel, jax.ShapeDtypeStruct((ROWS, WIDTH), BF16), [conv, gate, direct], [turned], name="gate"
    )
    return call(
        output_kernel,
        jax.ShapeDtypeStruct((ROWS, WIDTH), BF16),
        [*gather(gated), *columns],
        flops=2 * 64 << 20,
        name="output",
    )


def solution(mesh):
    return jax.shard_map(
        on_device,
        mesh=mesh,
        in_specs=(
            P("seq", "chan"),
            P(None, None, "chan"),
            P(None, None, "chan"),
            P("seq", "chan"),
            P("chan"),
            P("chan", None),
        ),
        out_specs=P("seq", "chan"),
        check_vma=False,
    )
```

```python
import functools
import math

import jax
import jax.numpy as jnp
import ml_dtypes
import numpy as np
from jax import lax
from jax.experimental import pallas as pl
from jax.experimental.pallas import tpu as pltpu
from jax.sharding import PartitionSpec as P


F32 = jnp.float32
BF16 = jnp.bfloat16
VMEM = pltpu.VMEM

SHARDS = 32
CHANS = 4
ROWS = 1024
WIDTH = 128
GROUP = 4
OUTER = 256
INNER = 128
LENGTH = OUTER * INNER


def halves(table):
    high = table.astype(ml_dtypes.bfloat16)
    low = (table - high.astype(np.float64)).astype(ml_dtypes.bfloat16)
    return high, low


@functools.lru_cache(None)
def tables():
    k1 = np.arange(OUTER)[:, None]
    a = np.arange(OUTER)[None, :]
    angle = 2 * math.pi / (4 * OUTER) * (a * (4 * k1 + 1) % (4 * OUTER))
    first = np.concatenate([np.cos(angle), -np.sin(angle)], 0)
    last = np.concatenate([np.cos(angle), -np.sin(angle)], 0).T / LENGTH
    p = np.arange(INNER)
    turn = 2 * math.pi / (4 * LENGTH) * (p[None, :] * (4 * k1 + 1) % (4 * LENGTH))
    twiddle = np.concatenate([np.cos(turn), np.sin(turn)], 1).astype(np.float32)
    phase = 2 * math.pi / INNER * (p[:, None] * p[None, :] % INNER)
    c, s = np.cos(phase), np.sin(phase)
    second = np.block([[c, -s], [s, c]])
    third = np.block([[c, s], [-s, c]])
    return twiddle, halves(first), halves(second), halves(third), halves(last)


def split(value):
    high = value.astype(BF16)
    return high, (value - high.astype(F32)).astype(BF16)


def dot(left, right):
    return jnp.dot(left, right, preferred_element_type=F32)


def dot3(left, right):
    (lh, ll), (rh, rl) = left, right
    return dot(lh, rh) + (dot(lh, rl) + dot(ll, rh))


def load_signal(ref, kind):
    rows = slice(kind * GROUP * 8, (kind + 1) * GROUP * 8)
    wide = ref[:, rows, :].astype(F32).reshape(SHARDS, GROUP, 8, INNER)
    return jnp.concatenate(
        [wide[:, c].reshape(OUTER, INNER).astype(BF16) for c in range(GROUP)], axis=1
    )


def forward(signal, tw, f_hi, f_lo, s_hi, s_lo):
    first = dot(f_hi[...], signal) + dot(f_lo[...], signal)
    cos, sin = tw[:, :INNER], tw[:, INNER:]
    rows = []
    for c in range(GROUP):
        re = first[:OUTER, c * INNER : (c + 1) * INNER]
        im = first[OUTER:, c * INNER : (c + 1) * INNER]
        rows.append(jnp.concatenate([re * cos + im * sin, im * cos - re * sin], axis=1))
    turned = jnp.concatenate(rows, axis=0)
    return dot3(split(turned), (s_hi[...], s_lo[...]))


def conv_kernel(sig, tw, f_hi, f_lo, s_hi, s_lo, t_hi, t_lo, l_hi, l_lo, out):
    spec = forward(load_signal(sig, 0), tw, f_hi, f_lo, s_hi, s_lo)
    mine = forward(load_signal(sig, 1), tw, f_hi, f_lo, s_hi, s_lo)
    mr, mi = mine[:, :INNER], mine[:, INNER:]
    hr, hi = spec[:, :INNER], spec[:, INNER:]
    product = jnp.concatenate([mr * hr - mi * hi, mr * hi + mi * hr], axis=1)
    back = dot3(split(product), (t_hi[...], t_lo[...]))
    cos, sin = tw[:, :INNER], tw[:, INNER:]
    res, ims = [], []
    for c in range(GROUP):
        re = back[c * OUTER : (c + 1) * OUTER, :INNER]
        im = back[c * OUTER : (c + 1) * OUTER, INNER:]
        res.append(re * cos - im * sin)
        ims.append(im * cos + re * sin)
    turned = jnp.concatenate(
        [jnp.concatenate(res, axis=1), jnp.concatenate(ims, axis=1)], axis=0
    )
    y = dot3((l_hi[...], l_lo[...]), split(turned))
    parts = [
        y[:, c * INNER : (c + 1) * INNER].reshape(SHARDS, 1, 8, INNER) for c in range(GROUP)
    ]
    wide = jnp.concatenate(parts, axis=1).reshape(SHARDS, GROUP * 8, INNER)
    out[...] = wide.astype(BF16)


def to_channels(value, scratch):
    for q in range(8):
        scratch[pl.ds(q, WIDTH, stride=8), :] = value[q * INNER : (q + 1) * INNER].T
    return scratch[...].reshape(SHARDS, GROUP * 8, INNER).astype(BF16)


def turn_kernel(value, out, scratch):
    out[...] = to_channels(value[...], scratch)


def project_kernel(me, t0, t1, t2, far, r0, r2, w, short_filter, skip, taps, out, gate, direct, ext, scratch):
    chan = me[0]
    first = me[1] == 0
    weights = jnp.concatenate(
        [w[pl.ds(pl.multiple_of((chan ^ r) * WIDTH, WIDTH), WIDTH), :] for r in range(CHANS)], axis=0
    )
    r1, r3 = far[ROWS + WIDTH : ROWS + WIDTH + 16], far[ROWS + WIDTH + 16 :]
    rim = jnp.concatenate([r0[...], r1, r2[...], r3], axis=1)
    rim = dot(rim, weights).astype(BF16).astype(F32)
    ext[:8, :] = jnp.where(first, 0.0, rim[8:])
    tokens = jnp.concatenate([t0[...], t1[...], t2[...], far[:ROWS]], axis=1)
    ext[8:, :] = dot(tokens, weights).astype(BF16).astype(F32)
    short = []
    for g in range(3):
        lanes = slice(g * WIDTH, (g + 1) * WIDTH)
        tap = [short_filter[j, g, :].reshape(1, WIDTH) for j in range(3)]
        short.append(
            tap[0] * ext[8:, lanes]
            + tap[1] * ext[7 : ROWS + 7, lanes]
            + tap[2] * ext[6 : ROWS + 6, lanes]
        )
    inner = short[0] * short[1]
    gate[...] = short[2]
    direct[...] = skip[...] * inner
    out[:, : GROUP * 8, :] = taps[...]
    out[:, GROUP * 8 :, :] = to_channels(inner, scratch)


def gate_kernel(conv, gate, direct, out, scratch):
    scratch[...] = conv[...].astype(F32).reshape(ROWS, WIDTH)
    for q in range(8):
        rows = slice(q * INNER, (q + 1) * INNER)
        back = scratch[pl.ds(q, WIDTH, stride=8), :].T
        out[rows, :] = (gate[rows, :] * (back + direct[rows, :])).astype(BF16)


def output_kernel(g0, g1, g2, g3, w0, w1, w2, w3, out):
    gated = jnp.concatenate([g0[...], g1[...], g2[...], g3[...]], axis=1)
    weights = jnp.concatenate([w0[...], w1[...], w2[...], w3[...]], axis=0)
    out[...] = dot(gated, weights).astype(BF16)


def call(kernel, out_shape, args, scratch=(), smem=0, flops=0, name=None, vmem=16):
    many = isinstance(out_shape, (list, tuple))
    specs = [pl.BlockSpec(memory_space=pltpu.SMEM)] * smem
    specs += [pl.BlockSpec(memory_space=VMEM)] * (len(args) - smem)
    outs = [pl.BlockSpec(memory_space=VMEM) for _ in out_shape] if many else pl.BlockSpec(memory_space=VMEM)
    moved = sum(x.size * x.dtype.itemsize for x in args)
    return pl.pallas_call(
        kernel,
        out_shape=out_shape,
        in_specs=specs,
        out_specs=outs,
        scratch_shapes=list(scratch),
        name=name,
        cost_estimate=pl.CostEstimate(flops=flops, bytes_accessed=moved, transcendentals=0),
        compiler_params=pltpu.CompilerParams(vmem_limit_bytes=vmem << 20),
    )(*args)


def swap(value, distance):
    return lax.ppermute(value, "chan", [(i, i ^ distance) for i in range(CHANS)])


def gather(value):
    near = swap(value, 1)
    far = swap(value, 2)
    return [value, near, far, swap(far, 1)]


def on_device(tokens, w_in, short_filter, long_filter, skip_gain, w_out):
    chan = lax.axis_index("chan")
    shard = lax.axis_index("seq")
    me = jnp.stack([chan, shard]).astype(jnp.int32)
    packed = jax.ShapeDtypeStruct((SHARDS, GROUP * 8, INNER), BF16)
    turned = VMEM((ROWS, WIDTH), F32)
    block = jax.ShapeDtypeStruct((ROWS, WIDTH), F32)

    tw, first, second, third, last = tables()
    tw = jnp.asarray(tw)
    first, second, third, last = [tuple(jnp.asarray(x) for x in t) for t in (first, second, third, last)]

    beyond = swap(tokens, 2)
    near = swap(tokens, 1)
    rims = []
    for r in (0, 2):
        route = [
            (s * CHANS + c, (s + 1) * CHANS + (c ^ r)) for s in range(SHARDS - 1) for c in range(CHANS)
        ]
        rims.append(lax.ppermute(tokens[-16:], ("seq", "chan"), route))
    pieces = [lax.dynamic_slice_in_dim(w_out, (chan ^ r) * WIDTH, WIDTH, axis=1) for r in range(CHANS)]
    columns = [pieces[0], swap(pieces[1], 1)]
    over = swap(jnp.concatenate([pieces[2], pieces[3]], axis=0), 2)
    columns.append(over[:WIDTH])
    weights = w_in.reshape(CHANS * WIDTH, 3 * WIDTH)
    taps = call(turn_kernel, packed, [long_filter], [turned], name="turn")
    load = jnp.concatenate([beyond, over[WIDTH:], *rims], axis=0)
    load, taps, weights, columns, near, rims = lax.optimization_barrier((load, taps, weights, columns, near, rims))
    far = swap(load, 1)
    columns.append(far[ROWS : ROWS + WIDTH])

    inner, gate, direct = call(
        project_kernel,
        [jax.ShapeDtypeStruct((SHARDS, 2 * GROUP * 8, INNER), BF16), block, block],
        [me, tokens, near, beyond, far, *rims, weights, short_filter, skip_gain.reshape(1, WIDTH), taps],
        [VMEM((ROWS + 8, 3 * WIDTH), F32), turned],
        smem=1,
        flops=2 * 200 << 20,
        name="project",
    )
    inner = lax.all_to_all(inner, "seq", 0, 0)
    conv = call(
        conv_kernel,
        packed,
        [inner, tw, *first, *second, *third, *last],
        flops=2 * 1060 << 20,
        name="conv",
        vmem=32,
    )
    conv = lax.all_to_all(conv, "seq", 0, 0)
    gated = call(
        gate_kernel, jax.ShapeDtypeStruct((ROWS, WIDTH), BF16), [conv, gate, direct], [turned], name="gate"
    )
    return call(
        output_kernel,
        jax.ShapeDtypeStruct((ROWS, WIDTH), BF16),
        [*gather(gated), *columns],
        flops=2 * 64 << 20,
        name="output",
    )


def solution(mesh):
    return jax.shard_map(
        on_device,
        mesh=mesh,
        in_specs=(
            P("seq", "chan"),
            P(None, None, "chan"),
            P(None, None, "chan"),
            P("seq", "chan"),
            P("chan"),
            P("chan", None),
        ),
        out_specs=P("seq", "chan"),
        check_vma=False,
    )
```

```python
import functools
import math

import jax
import jax.numpy as jnp
import ml_dtypes
import numpy as np
from jax import lax
from jax.experimental import pallas as pl
from jax.experimental.pallas import tpu as pltpu
from jax.sharding import PartitionSpec as P


F32 = jnp.float32
BF16 = jnp.bfloat16
VMEM = pltpu.VMEM

SHARDS = 32
CHANS = 4
ROWS = 1024
WIDTH = 128
GROUP = 4
OUTER = 256
INNER = 128
LENGTH = OUTER * INNER
SIG = GROUP * 8
EDGE = 8


def halves(table):
    high = table.astype(ml_dtypes.bfloat16)
    low = (table - high.astype(np.float64)).astype(ml_dtypes.bfloat16)
    return high, low


@functools.lru_cache(None)
def tables():
    k1 = np.arange(OUTER)[:, None]
    a = np.arange(OUTER)[None, :]
    angle = 2 * math.pi / (4 * OUTER) * (a * (4 * k1 + 1) % (4 * OUTER))
    first = np.concatenate([np.cos(angle), -np.sin(angle)], 0)
    last = np.concatenate([np.cos(angle), -np.sin(angle)], 0).T / LENGTH
    p = np.arange(INNER)
    turn = 2 * math.pi / (4 * LENGTH) * (p[None, :] * (4 * k1 + 1) % (4 * LENGTH))
    twiddle = np.concatenate([np.cos(turn), np.sin(turn)], 1).astype(np.float32)
    phase = 2 * math.pi / INNER * (p[:, None] * p[None, :] % INNER)
    c, s = np.cos(phase), np.sin(phase)
    second = np.block([[c, -s], [s, c]])
    third = np.block([[c, s], [-s, c]])
    return twiddle, halves(first), halves(second), halves(third), halves(last)


def split(value):
    high = value.astype(BF16)
    return high, (value - high.astype(F32)).astype(BF16)


def dot(left, right):
    return jnp.dot(left, right, preferred_element_type=F32)


def dot3(left, right):
    (lh, ll), (rh, rl) = left, right
    return dot(lh, rh) + (dot(lh, rl) + dot(ll, rh))


def load_signal(value):
    wide = value.reshape(SHARDS, GROUP, 8, INNER)
    return jnp.concatenate(
        [wide[:, c].reshape(OUTER, INNER).astype(BF16) for c in range(GROUP)], axis=1
    )


def forward(signal, tw, f_hi, f_lo, s_hi, s_lo):
    first = dot(f_hi[...], signal) + dot(f_lo[...], signal)
    cos, sin = tw[:, :INNER], tw[:, INNER:]
    rows = []
    for c in range(GROUP):
        re = first[:OUTER, c * INNER : (c + 1) * INNER]
        im = first[OUTER:, c * INNER : (c + 1) * INNER]
        rows.append(jnp.concatenate([re * cos + im * sin, im * cos - re * sin], axis=1))
    turned = jnp.concatenate(rows, axis=0)
    return dot3(split(turned), (s_hi[...], s_lo[...]))


def conv_kernel(
    sig, coef, tw, f_hi, f_lo, s_hi, s_lo, t_hi, t_lo, l_hi, l_lo, out, scratch, pairs, shifted
):
    spec = forward(load_signal(sig[:, :SIG, :].astype(F32)), tw, f_hi, f_lo, s_hi, s_lo)
    pairs[...] = sig[:, 2 * SIG :, :].astype(F32).reshape(2 * WIDTH, INNER)
    heads, tails = pairs[pl.ds(0, WIDTH, stride=2), :], pairs[pl.ds(1, WIDTH, stride=2), :]
    shifted[:8, :] = jnp.zeros((8, INNER), F32)
    shifted[8:, :] = tails
    before = shifted[8 - GROUP : 8 - GROUP + WIDTH, :]
    pairs[pl.ds(0, WIDTH, stride=2), :] = before
    out[:, SIG:, :] = pairs[...].reshape(SHARDS, EDGE, INNER).astype(BF16)
    terms = (heads + before) * coef[...]
    short = terms + pltpu.roll(terms, INNER - 2, 1) + pltpu.roll(terms, INNER - 4, 1)
    edge = short * pltpu.roll(short, INNER - 6, 1)
    scratch[...] = sig[:, SIG : 2 * SIG, :].astype(F32).reshape(ROWS, INNER)
    lane = lax.broadcasted_iota(jnp.int32, (WIDTH, INNER), 1)
    opening = scratch[pl.ds(0, WIDTH, stride=8), :]
    scratch[pl.ds(0, WIDTH, stride=8), :] = jnp.where(lane < 2, edge, opening)
    mine = forward(load_signal(scratch[...]), tw, f_hi, f_lo, s_hi, s_lo)
    mr, mi = mine[:, :INNER], mine[:, INNER:]
    hr, hi = spec[:, :INNER], spec[:, INNER:]
    product = jnp.concatenate([mr * hr - mi * hi, mr * hi + mi * hr], axis=1)
    back = dot3(split(product), (t_hi[...], t_lo[...]))
    cos, sin = tw[:, :INNER], tw[:, INNER:]
    res, ims = [], []
    for c in range(GROUP):
        re = back[c * OUTER : (c + 1) * OUTER, :INNER]
        im = back[c * OUTER : (c + 1) * OUTER, INNER:]
        res.append(re * cos - im * sin)
        ims.append(im * cos + re * sin)
    turned = jnp.concatenate(
        [jnp.concatenate(res, axis=1), jnp.concatenate(ims, axis=1)], axis=0
    )
    y = dot3((l_hi[...], l_lo[...]), split(turned))
    parts = [
        y[:, c * INNER : (c + 1) * INNER].reshape(SHARDS, 1, 8, INNER) for c in range(GROUP)
    ]
    wide = jnp.concatenate(parts, axis=1).reshape(SHARDS, GROUP * 8, INNER)
    out[:, :SIG, :] = wide.astype(BF16)


def to_channels(value, scratch):
    for q in range(8):
        scratch[pl.ds(q, WIDTH, stride=8), :] = value[q * INNER : (q + 1) * INNER].T
    return scratch[...].reshape(SHARDS, GROUP * 8, INNER).astype(BF16)


def turn_kernel(value, out, scratch):
    out[...] = to_channels(value[...], scratch)


def project_kernel(
    me, t0, t1, t2, t3, w, short_filter, skip, taps, out, gate, direct, edge, ext, scratch, pairs, square
):
    chan = me[0]
    order = [pl.ds(pl.multiple_of((chan ^ r) * WIDTH, WIDTH), WIDTH) for r in range(CHANS)]
    weights = jnp.concatenate(
        [jnp.concatenate([w[g, rows, :] for rows in order], axis=0) for g in range(3)], axis=1
    )
    tokens = jnp.concatenate([t0[...], t1[...], t2[...], t3[...]], axis=1)
    ext[:8, :] = jnp.zeros((8, 3 * WIDTH), F32)
    ext[8:, :] = dot(tokens, weights).astype(BF16).astype(F32)
    short = []
    for g in range(3):
        lanes = slice(g * WIDTH, (g + 1) * WIDTH)
        tap = [short_filter[j, g, :].reshape(1, WIDTH) for j in range(3)]
        short.append(
            tap[0] * ext[8:, lanes]
            + tap[1] * ext[7 : ROWS + 7, lanes]
            + tap[2] * ext[6 : ROWS + 6, lanes]
        )
    inner = short[0] * short[1]
    gate[...] = short[2]
    direct[...] = skip[...] * inner
    edge[:8, :] = short[0][:8]
    edge[8:, :] = short[1][:8]
    out[:, :SIG, :] = taps[...]
    out[:, SIG : 2 * SIG, :] = to_channels(inner, scratch)
    square[...] = jnp.zeros((INNER, WIDTH), F32)
    for g in range(2):
        lanes = slice(g * WIDTH, (g + 1) * WIDTH)
        square[6 * g : 6 * g + 2, :] = ext[8:10, lanes]
        square[6 * g + 3 : 6 * g + 4, :] = ext[8:9, lanes]
    pairs[pl.ds(0, WIDTH, stride=2), :] = square[...].T
    square[...] = jnp.zeros((INNER, WIDTH), F32)
    for g in range(3):
        lanes = slice(g * WIDTH, (g + 1) * WIDTH)
        square[6 * g + 2 : 6 * g + 3, :] = ext[ROWS + 7 : ROWS + 8, lanes]
        square[6 * g + 4 : 6 * g + 6, :] = ext[ROWS + 6 : ROWS + 8, lanes]
    pairs[pl.ds(1, WIDTH, stride=2), :] = square[...].T
    out[:, 2 * SIG :, :] = pairs[...].reshape(SHARDS, EDGE, INNER).astype(BF16)


def gate_kernel(conv, gate, direct, edge, short_filter, skip, out, scratch, pairs, square):
    scratch[...] = conv[:, :SIG, :].astype(F32).reshape(ROWS, WIDTH)
    pairs[...] = conv[:, SIG:, :].astype(F32).reshape(2 * WIDTH, INNER)
    square[...] = pairs[pl.ds(0, WIDTH, stride=2), :].T
    short = []
    for g, start in enumerate((edge[:2, :], edge[8:10, :], gate[:2, :])):
        tap = [short_filter[j, g, :].reshape(1, WIDTH) for j in range(3)]
        short.append(
            start + tap[1] * square[6 * g + 2 : 6 * g + 4, :] + tap[2] * square[6 * g + 4 : 6 * g + 6, :]
        )
    inner = short[0] * short[1]
    for q in range(8):
        rows = slice(q * INNER, (q + 1) * INNER)
        back = scratch[pl.ds(q, WIDTH, stride=8), :].T
        out[rows, :] = (gate[rows, :] * (back + direct[rows, :])).astype(BF16)
        if q == 0:
            gates = jnp.concatenate([short[2], gate[2:16, :]], axis=0)
            directs = jnp.concatenate([skip[...] * inner, direct[2:16, :]], axis=0)
            out[:16, :] = (gates * (back[:16] + directs)).astype(BF16)


def output_kernel(g0, g1, g2, g3, w0, w1, w2, w3, out):
    gated = jnp.concatenate([g0[...], g1[...], g2[...], g3[...]], axis=1)
    weights = jnp.concatenate([w0[...], w1[...], w2[...], w3[...]], axis=0)
    out[...] = dot(gated, weights).astype(BF16)


def call(kernel, out_shape, args, scratch=(), smem=0, flops=0, vmem=16):
    many = isinstance(out_shape, (list, tuple))
    specs = [pl.BlockSpec(memory_space=pltpu.SMEM)] * smem
    specs += [pl.BlockSpec(memory_space=VMEM)] * (len(args) - smem)
    outs = [pl.BlockSpec(memory_space=VMEM) for _ in out_shape] if many else pl.BlockSpec(memory_space=VMEM)
    moved = sum(x.size * x.dtype.itemsize for x in args)
    return pl.pallas_call(
        kernel,
        out_shape=out_shape,
        in_specs=specs,
        out_specs=outs,
        scratch_shapes=list(scratch),
        cost_estimate=pl.CostEstimate(flops=flops, bytes_accessed=moved, transcendentals=0),
        compiler_params=pltpu.CompilerParams(vmem_limit_bytes=vmem << 20),
    )(*args)


def swap(value, distance):
    return lax.ppermute(value, "chan", [(i, i ^ distance) for i in range(CHANS)])


def operator(tokens, w_in, short_filter, long_filter, skip_gain, w_out):
    chan = lax.axis_index("chan")
    shard = lax.axis_index("seq")
    me = jnp.stack([chan, shard]).astype(jnp.int32)
    turned = VMEM((ROWS, WIDTH), F32)
    pairs, square = VMEM((2 * WIDTH, INNER), F32), VMEM((INNER, WIDTH), F32)
    block = jax.ShapeDtypeStruct((ROWS, WIDTH), F32)

    tw, first, second, third, last = tables()
    tw = jnp.asarray(tw)
    first, second, third, last = [tuple(jnp.asarray(x) for x in t) for t in (first, second, third, last)]

    beyond = swap(tokens, 2)
    near = swap(tokens, 1)
    near, w_out, own_filter = lax.optimization_barrier((near, w_out, short_filter))
    pieces = [lax.dynamic_slice_in_dim(w_out, (chan ^ r) * WIDTH, WIDTH, axis=1) for r in range(CHANS)]
    columns = [pieces[0], swap(pieces[1], 1)]
    over = jnp.concatenate([pieces[2], pieces[3]], axis=0)
    coef = lax.dynamic_slice_in_dim(own_filter, shard * GROUP, GROUP, axis=2)[:, :2, :]
    coef = jnp.repeat(coef.transpose(2, 1, 0).reshape(GROUP, 6), 2, axis=1)
    coef = jnp.tile(jnp.pad(coef, ((0, 0), (0, INNER - 12))), (SHARDS, 1))
    weights = w_in.transpose(1, 0, 2)
    taps = call(
        turn_kernel, jax.ShapeDtypeStruct((SHARDS, SIG, INNER), BF16), [long_filter], [turned]
    )
    beyond, taps, weights, columns, near, coef, over = lax.optimization_barrier(
        (beyond, taps, weights, columns, near, coef, over)
    )
    far = swap(beyond, 1)
    over = swap(over, 2)

    skip = skip_gain.reshape(1, WIDTH)
    inner, gate, direct, edge = call(
        project_kernel,
        [
            jax.ShapeDtypeStruct((SHARDS, 2 * SIG + EDGE, INNER), BF16),
            block,
            block,
            jax.ShapeDtypeStruct((16, WIDTH), F32),
        ],
        [me, tokens, near, beyond, far, weights, short_filter, skip, taps],
        [VMEM((ROWS + 8, 3 * WIDTH), F32), turned, pairs, square],
        smem=1,
        flops=2 * 200 << 20,
    )
    inner = lax.all_to_all(inner, "seq", 0, 0)
    conv = call(
        conv_kernel,
        jax.ShapeDtypeStruct((SHARDS, SIG + EDGE, INNER), BF16),
        [inner, coef, tw, *first, *second, *third, *last],
        [turned, pairs, VMEM((WIDTH + 8, INNER), F32)],
        flops=2 * 1060 << 20,
        vmem=32,
    )
    conv = lax.all_to_all(conv, "seq", 0, 0)
    gated = call(
        gate_kernel,
        jax.ShapeDtypeStruct((ROWS, WIDTH), BF16),
        [conv, gate, direct, edge, short_filter, skip],
        [turned, pairs, square],
    )
    beyond = swap(gated, 2)
    near = swap(gated, 1)
    over, near = lax.optimization_barrier((over, near))
    last_column = swap(over[WIDTH:], 1)
    beyond, last_column = lax.optimization_barrier((beyond, last_column))
    columns += [over[:WIDTH], last_column]
    return call(
        output_kernel,
        jax.ShapeDtypeStruct((ROWS, WIDTH), BF16),
        [gated, near, beyond, swap(beyond, 1), *columns],
        flops=2 * 64 << 20,
    )


def solution(mesh):
    return jax.shard_map(
        operator,
        mesh=mesh,
        in_specs=(
            P("seq", "chan"),
            P(None, None, "chan"),
            P(None, None, "chan"),
            P("seq", "chan"),
            P("chan"),
            P("chan", None),
        ),
        out_specs=P("seq", "chan"),
        check_vma=False,
    )
```

```python
import functools
import math

import jax
import jax.numpy as jnp
import ml_dtypes
import numpy as np
from jax import lax
from jax.experimental import pallas as pl
from jax.experimental.pallas import tpu as pltpu
from jax.sharding import PartitionSpec as P


F32 = jnp.float32
BF16 = jnp.bfloat16
VMEM = pltpu.VMEM

SHARDS = 32
CHANS = 4
ROWS = 1024
WIDTH = 128
GROUP = 4
OUTER = 256
INNER = 128
LENGTH = OUTER * INNER
SIG = GROUP * 8
PARTS = 4
EDGE = 8


def halves(table):
    high = table.astype(ml_dtypes.bfloat16)
    low = (table - high.astype(np.float64)).astype(ml_dtypes.bfloat16)
    return high, low


@functools.lru_cache(None)
def tables():
    k1 = np.arange(OUTER)[:, None]
    a = np.arange(OUTER)[None, :]
    angle = 2 * math.pi / (4 * OUTER) * (a * (4 * k1 + 1) % (4 * OUTER))
    first = np.concatenate([np.cos(angle), -np.sin(angle)], 0)
    last = np.concatenate([np.cos(angle), -np.sin(angle)], 0).T / LENGTH
    p = np.arange(INNER)
    turn = 2 * math.pi / (4 * LENGTH) * (p[None, :] * (4 * k1 + 1) % (4 * LENGTH))
    twiddle = np.concatenate([np.cos(turn), np.sin(turn)], 1).astype(np.float32)
    phase = 2 * math.pi / INNER * (p[:, None] * p[None, :] % INNER)
    c, s = np.cos(phase), np.sin(phase)
    second = np.block([[c, -s], [s, c]])
    third = np.block([[c, s], [-s, c]])
    return twiddle, halves(first), halves(second), halves(third), halves(last)


def split(value):
    high = value.astype(BF16)
    return high, (value - high.astype(F32)).astype(BF16)


def dot(left, right):
    return jnp.dot(left, right, preferred_element_type=F32)


def dot3(left, right):
    (lh, ll), (rh, rl) = left, right
    return dot(jnp.concatenate([lh, lh, ll], axis=1), jnp.concatenate([rl, rh, rh], axis=0))


def load_signal(value):
    wide = value.reshape(SHARDS, GROUP, 8, INNER)
    return jnp.concatenate(
        [wide[:, c].reshape(OUTER, INNER).astype(BF16) for c in range(GROUP)], axis=1
    )


def forward(signal, tw, f_hi, f_lo, s_hi, s_lo):
    first = dot(
        jnp.concatenate([f_lo[...], f_hi[...]], axis=1), jnp.concatenate([signal, signal], axis=0)
    )
    cos, sin = tw[:, :INNER], tw[:, INNER:]
    rows = []
    for c in range(GROUP):
        re = first[:OUTER, c * INNER : (c + 1) * INNER]
        im = first[OUTER:, c * INNER : (c + 1) * INNER]
        rows.append(jnp.concatenate([re * cos + im * sin, im * cos - re * sin], axis=1))
    turned = jnp.concatenate(rows, axis=0)
    return dot3(split(turned), (s_hi[...], s_lo[...]))


def conv_kernel(
    sig, coef, tw, f_hi, f_lo, s_hi, s_lo, t_hi, t_lo, l_hi, l_lo, out, scratch, pairs, shifted
):
    spec = forward(load_signal(sig[:, :SIG, :].astype(F32)), tw, f_hi, f_lo, s_hi, s_lo)
    pairs[...] = sig[:, 2 * SIG :, :].astype(F32).reshape(2 * WIDTH, INNER)
    heads, tails = pairs[pl.ds(0, WIDTH, stride=2), :], pairs[pl.ds(1, WIDTH, stride=2), :]
    shifted[:8, :] = jnp.zeros((8, INNER), F32)
    shifted[8:, :] = tails
    before = shifted[8 - GROUP : 8 - GROUP + WIDTH, :]
    pairs[pl.ds(0, WIDTH, stride=2), :] = before
    out[:, SIG:, :] = pairs[...].reshape(SHARDS, EDGE, INNER).astype(BF16)
    terms = (heads + before) * coef[...]
    short = terms + pltpu.roll(terms, INNER - 2, 1) + pltpu.roll(terms, INNER - 4, 1)
    edge = short * pltpu.roll(short, INNER - 6, 1)
    scratch[...] = sig[:, SIG : 2 * SIG, :].astype(F32).reshape(ROWS, INNER)
    lane = lax.broadcasted_iota(jnp.int32, (WIDTH, INNER), 1)
    opening = scratch[pl.ds(0, WIDTH, stride=8), :]
    scratch[pl.ds(0, WIDTH, stride=8), :] = jnp.where(lane < 2, edge, opening)
    mine = forward(load_signal(scratch[...]), tw, f_hi, f_lo, s_hi, s_lo)
    mr, mi = mine[:, :INNER], mine[:, INNER:]
    hr, hi = spec[:, :INNER], spec[:, INNER:]
    product = jnp.concatenate([mr * hr - mi * hi, mr * hi + mi * hr], axis=1)
    back = dot3(split(product), (t_hi[...], t_lo[...]))
    cos, sin = tw[:, :INNER], tw[:, INNER:]
    res, ims = [], []
    for c in range(GROUP):
        re = back[c * OUTER : (c + 1) * OUTER, :INNER]
        im = back[c * OUTER : (c + 1) * OUTER, INNER:]
        res.append(re * cos - im * sin)
        ims.append(im * cos + re * sin)
    turned = jnp.concatenate(
        [jnp.concatenate(res, axis=1), jnp.concatenate(ims, axis=1)], axis=0
    )
    y = dot3((l_hi[...], l_lo[...]), split(turned))
    parts = [
        y[:, c * INNER : (c + 1) * INNER].reshape(SHARDS, 1, 8, INNER) for c in range(GROUP)
    ]
    wide = jnp.concatenate(parts, axis=1).reshape(SHARDS, GROUP * 8, INNER)
    out[:, :SIG, :] = wide.astype(BF16)


def to_channels(value, scratch):
    for q in range(8):
        scratch[pl.ds(q, WIDTH, stride=8), :] = value[q * INNER : (q + 1) * INNER].T
    return scratch[...].reshape(SHARDS, GROUP * 8, INNER).astype(BF16)


def turn_kernel(value, out, scratch):
    out[...] = to_channels(value[...], scratch)


def project_kernel(
    me, t0, t1, t2, t3, w, short_filter, skip, taps, out, gate, direct, edge, ext, scratch, pairs, square
):
    chan = me[0]
    order = [pl.ds(pl.multiple_of((chan ^ r) * WIDTH, WIDTH), WIDTH) for r in range(CHANS)]
    weights = jnp.concatenate(
        [jnp.concatenate([w[g, rows, :] for rows in order], axis=0) for g in range(3)], axis=1
    )
    tokens = jnp.concatenate([t0[...], t1[...], t2[...], t3[...]], axis=1)
    ext[:8, :] = jnp.zeros((8, 3 * WIDTH), F32)
    ext[8:, :] = dot(tokens, weights).astype(BF16).astype(F32)
    short = []
    for g in range(3):
        lanes = slice(g * WIDTH, (g + 1) * WIDTH)
        tap = [short_filter[j, g, :].reshape(1, WIDTH) for j in range(3)]
        short.append(
            tap[0] * ext[8:, lanes]
            + tap[1] * ext[7 : ROWS + 7, lanes]
            + tap[2] * ext[6 : ROWS + 6, lanes]
        )
    inner = short[0] * short[1]
    gate[...] = short[2]
    direct[...] = skip[...] * inner
    edge[:8, :] = short[0][:8]
    edge[8:, :] = short[1][:8]
    out[:, :SIG, :] = taps[...]
    out[:, SIG : 2 * SIG, :] = to_channels(inner, scratch)
    square[...] = jnp.zeros((INNER, WIDTH), F32)
    for g in range(2):
        lanes = slice(g * WIDTH, (g + 1) * WIDTH)
        square[6 * g : 6 * g + 2, :] = ext[8:10, lanes]
        square[6 * g + 3 : 6 * g + 4, :] = ext[8:9, lanes]
    pairs[pl.ds(0, WIDTH, stride=2), :] = square[...].T
    square[...] = jnp.zeros((INNER, WIDTH), F32)
    for g in range(3):
        lanes = slice(g * WIDTH, (g + 1) * WIDTH)
        square[6 * g + 2 : 6 * g + 3, :] = ext[ROWS + 7 : ROWS + 8, lanes]
        square[6 * g + 4 : 6 * g + 6, :] = ext[ROWS + 6 : ROWS + 8, lanes]
    pairs[pl.ds(1, WIDTH, stride=2), :] = square[...].T
    out[:, 2 * SIG :, :] = pairs[...].reshape(SHARDS, EDGE, INNER).astype(BF16)


def gate_kernel(conv, gate, direct, edge, short_filter, skip, out, scratch, pairs, square):
    scratch[...] = conv[:, :SIG, :].astype(F32).reshape(ROWS, WIDTH)
    pairs[...] = conv[:, SIG:, :].astype(F32).reshape(2 * WIDTH, INNER)
    square[...] = pairs[pl.ds(0, WIDTH, stride=2), :].T
    short = []
    for g, start in enumerate((edge[:2, :], edge[8:10, :], gate[:2, :])):
        tap = [short_filter[j, g, :].reshape(1, WIDTH) for j in range(3)]
        short.append(
            start + tap[1] * square[6 * g + 2 : 6 * g + 4, :] + tap[2] * square[6 * g + 4 : 6 * g + 6, :]
        )
    inner = short[0] * short[1]
    for q in range(8):
        rows = slice(q * INNER, (q + 1) * INNER)
        back = scratch[pl.ds(q, WIDTH, stride=8), :].T
        out[rows, :] = (gate[rows, :] * (back + direct[rows, :])).astype(BF16)
        if q == 0:
            gates = jnp.concatenate([short[2], gate[2:16, :]], axis=0)
            directs = jnp.concatenate([skip[...] * inner, direct[2:16, :]], axis=0)
            out[:16, :] = (gates * (back[:16] + directs)).astype(BF16)


def output_kernel(g0, g1, g2, g3, w0, w1, w2, w3, out, held, sems):
    weights = jnp.concatenate([w0[...], w1[...], w2[...], w3[...]], axis=0)
    copies = []
    for part in range(PARTS):
        rows = slice(part * ROWS // PARTS, (part + 1) * ROWS // PARTS)
        gated = jnp.concatenate([g[rows, :] for g in (g0, g1, g2, g3)], axis=1)
        held[rows, :] = dot(gated, weights).astype(BF16)
        copies.append(pltpu.make_async_copy(held.at[rows], out.at[rows], sems.at[part]))
        copies[-1].start()
    for copy in copies:
        copy.wait()


def call(kernel, out_shape, args, scratch=(), smem=0, flops=0, vmem=16, out_space=VMEM):
    many = isinstance(out_shape, (list, tuple))
    specs = [pl.BlockSpec(memory_space=pltpu.SMEM)] * smem
    specs += [pl.BlockSpec(memory_space=VMEM)] * (len(args) - smem)
    outs = [pl.BlockSpec(memory_space=VMEM) for _ in out_shape] if many else pl.BlockSpec(memory_space=out_space)
    moved = sum(x.size * x.dtype.itemsize for x in args)
    return pl.pallas_call(
        kernel,
        out_shape=out_shape,
        in_specs=specs,
        out_specs=outs,
        scratch_shapes=list(scratch),
        cost_estimate=pl.CostEstimate(flops=flops, bytes_accessed=moved, transcendentals=0),
        compiler_params=pltpu.CompilerParams(vmem_limit_bytes=vmem << 20),
    )(*args)


def swap(value, distance):
    return lax.ppermute(value, "chan", [(i, i ^ distance) for i in range(CHANS)])


def operator(tokens, w_in, short_filter, long_filter, skip_gain, w_out):
    chan = lax.axis_index("chan")
    shard = lax.axis_index("seq")
    me = jnp.stack([chan, shard]).astype(jnp.int32)
    turned = VMEM((ROWS, WIDTH), F32)
    pairs, square = VMEM((2 * WIDTH, INNER), F32), VMEM((INNER, WIDTH), F32)
    block = jax.ShapeDtypeStruct((ROWS, WIDTH), F32)

    tw, first, second, third, last = tables()
    tw = jnp.asarray(tw)
    first, second, third, last = [tuple(jnp.asarray(x) for x in t) for t in (first, second, third, last)]

    beyond = swap(tokens, 2)
    near = swap(tokens, 1)
    near, w_out, own_filter = lax.optimization_barrier((near, w_out, short_filter))
    pieces = [lax.dynamic_slice_in_dim(w_out, (chan ^ r) * WIDTH, WIDTH, axis=1) for r in range(CHANS)]
    columns = [pieces[0], swap(pieces[1], 1)]
    over = jnp.concatenate([pieces[2], pieces[3]], axis=0)
    coef = lax.dynamic_slice_in_dim(own_filter, shard * GROUP, GROUP, axis=2)[:, :2, :]
    coef = jnp.repeat(coef.transpose(2, 1, 0).reshape(GROUP, 6), 2, axis=1)
    coef = jnp.tile(jnp.pad(coef, ((0, 0), (0, INNER - 12))), (SHARDS, 1))
    weights = w_in.transpose(1, 0, 2)
    taps = call(
        turn_kernel, jax.ShapeDtypeStruct((SHARDS, SIG, INNER), BF16), [long_filter], [turned]
    )
    beyond, taps, weights, columns, near, coef, over = lax.optimization_barrier(
        (beyond, taps, weights, columns, near, coef, over)
    )
    far = swap(beyond, 1)
    over = swap(over, 2)

    skip = skip_gain.reshape(1, WIDTH)
    inner, gate, direct, edge = call(
        project_kernel,
        [
            jax.ShapeDtypeStruct((SHARDS, 2 * SIG + EDGE, INNER), BF16),
            block,
            block,
            jax.ShapeDtypeStruct((16, WIDTH), F32),
        ],
        [me, tokens, near, beyond, far, weights, short_filter, skip, taps],
        [VMEM((ROWS + 8, 3 * WIDTH), F32), turned, pairs, square],
        smem=1,
        flops=2 * 200 << 20,
    )
    inner = lax.all_to_all(inner, "seq", 0, 0)
    conv = call(
        conv_kernel,
        jax.ShapeDtypeStruct((SHARDS, SIG + EDGE, INNER), BF16),
        [inner, coef, tw, *first, *second, *third, *last],
        [turned, pairs, VMEM((WIDTH + 8, INNER), F32)],
        flops=2 * 1060 << 20,
        vmem=32,
    )
    conv = lax.all_to_all(conv, "seq", 0, 0)
    gated = call(
        gate_kernel,
        jax.ShapeDtypeStruct((ROWS, WIDTH), BF16),
        [conv, gate, direct, edge, short_filter, skip],
        [turned, pairs, square],
    )
    beyond = swap(gated, 2)
    near = swap(gated, 1)
    over, near = lax.optimization_barrier((over, near))
    last_column = swap(over[WIDTH:], 1)
    beyond, last_column = lax.optimization_barrier((beyond, last_column))
    columns += [over[:WIDTH], last_column]
    return call(
        output_kernel,
        jax.ShapeDtypeStruct((ROWS, WIDTH), BF16),
        [gated, near, beyond, swap(beyond, 1), *columns],
        [VMEM((ROWS, WIDTH), BF16), pltpu.SemaphoreType.DMA((PARTS,))],
        out_space=pl.ANY,
        flops=2 * 64 << 20,
    )


def solution(mesh):
    return jax.shard_map(
        operator,
        mesh=mesh,
        in_specs=(
            P("seq", "chan"),
            P(None, None, "chan"),
            P(None, None, "chan"),
            P("seq", "chan"),
            P("chan"),
            P("chan", None),
        ),
        out_specs=P("seq", "chan"),
        check_vma=False,
    )
```
